32 devices in a mesh: real: 2 (over y), tm: 4 (over z), wafer: 4 (over x, core).
Axes of the slice: x: 2, y: 2, z: 4, core: 2. Of those that a mesh axis runs over, the one named last changes fastest.
Arguments:
- tod: float32 [8192, 4096], P(('real', 'wafer'), 'tm'), parts along dimension 0, may hold values from -6 to 6
- inv_white: float32 [4096, 8], P('wafer'), may hold values from 0.5 to 2
- modes: float32 [4096, 128], P('wafer'), may hold values from -6 to 6
- mode_counts: int32 [8], replicated, may hold values from 8 to 16, as said below
- core: float32 [8, 16, 16], replicated, may hold values from -0.0017089844 to 0.0017089844
- block_coef: float32 [8, 16], replicated, may hold values from -0.109375 to 0.109375
- block_ids: int32 [4096], P('wafer'), may hold values from 0 to 15
- band_edges: int32 [9], replicated, may hold values from 0 to 256, as said below
Outputs:
- filtered: float32 [8192, 4096], P(('real', 'wafer'), 'tm'), parts along dimension 0
The draws below stay inside these ranges and needn't reach their ends.
There are 2 independent parts, one for each index of `real`. The reference program is written for one: setup_inputs(seed, part) draws one part's arguments, and reference() takes and returns one part's arrays. A program takes and returns all parts, laid end to end along the dimension named above; an argument that names none is the same for every part. Nothing has to cross between parts.
Inputs may be any that keep to these rules, and one draw needn't show every extreme that they name: band_edges[0] = 0 and band_edges[8] = 256, strictly rising; every band holds at least 16 bins. `mode_counts`: some band uses all 16 eigenvectors.
All inputs are finite; a program needn't handle non-finite values.
Results may differ from the reference program's by a relative error of at most 0.0003.
Values sent between devices are 32-bit elements; how exact they have to be, the bound alone decides.
No kernel may reach another device: no remote copies, remote signals or barrier semaphores. Data moves between devices by JAX's collectives and lax.ppermute only.
A program may use at most 128 MiB of HBM per device.

```python
import math
import jax
import jax.numpy as jnp
from jax import lax

SEGS = 4
STEP = 256
TAIL = 256
BANDS = 8
KMAX = 16
NBLK = 16
SEGLEN = 512
BINS = 256
DETS = 4096
SAMPLES = 4096
N_TM = 4


def draw_band_edges(key, part):
    least = BINS // (2 * BANDS)
    spare = BINS - BANDS * least
    cuts = jnp.sort(jax.random.randint(key, (BANDS - 1,), 0, spare + 1))
    bounds = jnp.concatenate([jnp.zeros((1,), jnp.int32), cuts.astype(jnp.int32), jnp.full((1,), spare, jnp.int32)])
    widths = bounds[1:] - bounds[:-1] + least
    edges = jnp.concatenate([jnp.zeros((1,), jnp.int32), jnp.cumsum(widths).astype(jnp.int32)])
    return edges.astype(jnp.int32)


def draw_mode_counts(key, part):
    counts = jax.random.randint(key, (BANDS,), KMAX // 2, KMAX + 1)
    chosen = jax.random.randint(jax.random.fold_in(key, 7), (), 0, BANDS)
    counts = jnp.where(jnp.arange(BANDS, dtype=jnp.int32) == chosen, KMAX, counts)
    return counts.astype(jnp.int32)


def with_ends(values, rng, low, top_value):
    longest = values.shape.index(max(values.shape))
    spots = []
    for shift in (0, 1):
        where = [jax.random.randint(jax.random.fold_in(rng, axis), (), 0, length) for axis, length in enumerate(values.shape)]
        where[longest] = (where[longest] + shift) % values.shape[longest]
        spots.append(tuple(where))
    return values.at[spots[0]].set(low).at[spots[1]].set(top_value)


def block_levels(key, extent, split, low, top_value):
    factor_of, own = 1.0, jax.random.fold_in(key, 6)
    for axis_at, parts in split:
        steps = jnp.exp(jax.random.uniform(jax.random.fold_in(own, axis_at), (parts,), jnp.float32, low / len(split), top_value / len(split)))
        factor_of = factor_of * jnp.repeat(steps, extent[axis_at] // parts).reshape([-1 if axis == axis_at else 1 for axis in range(len(extent))])
    return factor_of


def centred(key, extent, deviation, most, split=(), held_as=jnp.bfloat16):
    loudness = block_levels(key, extent, split, -0.22, 0.18) if split else 1.0
    array = jax.random.normal(key, extent, jnp.float32) * deviation * loudness
    return jnp.minimum(jnp.maximum(array, -most), most).astype(held_as)


def setup_inputs(seed: int = 0, part: int = 0) -> dict:
    splits = jax.random.split(jax.random.key(seed), 9)
    own_keys = jax.random.split(jax.random.fold_in(splits[8], part), 9)
    return {
        "tod": centred(own_keys[0], (DETS, SAMPLES), 1.0, 6.0, ((0, 4), (1, 4)), jnp.float32),
        "inv_white": jnp.clip(jnp.exp(math.log(2.0) - 1.3862944 * jax.random.uniform(splits[1], (DETS, BANDS), jnp.float32) ** block_levels(splits[1], (DETS, BANDS), ((0, 4),), -0.2, 0.2)), 0.5, 2.0),
        "modes": centred(splits[2], (DETS, BANDS * KMAX), 1.0, 6.0, ((0, 4),), jnp.float32),
        "mode_counts": draw_mode_counts(jax.random.fold_in(splits[8], 71), part),
        "core": centred(splits[4], (BANDS, KMAX, KMAX), (11 * KMAX * KMAX * DETS) ** -0.5, 0.0017089844, (), jnp.float32),
        "block_coef": centred(splits[5], (BANDS, NBLK), (11 * DETS // NBLK) ** -0.5, 0.109375, (), jnp.float32),
        "block_ids": with_ends(jax.random.randint(splits[6], (DETS,), 0, NBLK), jax.random.fold_in(splits[6], 1), 0, NBLK - 1).astype(jnp.int32),
        "band_edges": draw_band_edges(jax.random.fold_in(splits[8], 71), part),
    }


highest = lax.Precision.HIGHEST


def make_masks(band_edges):
    bin_idx = jnp.arange(BINS, dtype=jnp.int32)
    lower = band_edges[:-1].astype(jnp.int32)
    upper = band_edges[1:].astype(jnp.int32)
    inside = (bin_idx[None, :] >= lower[:, None]) & (bin_idx[None, :] < upper[:, None])
    return inside.astype(jnp.float32)


def reference(tod, inv_white, modes, mode_counts, core, block_coef, block_ids, band_edges):
    band_mask = make_masks(band_edges)
    mask_two = jnp.concatenate([band_mask, band_mask], 1)
    weight_bins = jnp.dot(inv_white, band_mask, precision=highest)
    weight_two = jnp.concatenate([weight_bins, weight_bins], 1)
    block_weight = jnp.dot(block_coef.T, band_mask, precision=highest)
    block_two = jnp.concatenate([block_weight, block_weight], 1)
    column_keep = (jnp.arange(KMAX, dtype=jnp.int32)[None, :] < mode_counts[:, None]).astype(jnp.float32).reshape(-1)
    live_modes = modes * column_keep[None, :]
    members = (block_ids[:, None] == jnp.arange(NBLK, dtype=jnp.int32)[None, :]).astype(jnp.float32)
    seg_total = SEGS * N_TM
    padded = jnp.concatenate([jnp.zeros((DETS, TAIL), jnp.float32), tod], 1)

    def one_segment(segment):
        start = (segment * STEP).astype(jnp.int32)
        piece = lax.dynamic_slice_in_dim(padded, start, SEGLEN, 1)
        freq = jnp.fft.rfft(piece, axis=1)[:, :BINS]
        plain = jnp.concatenate([jnp.real(freq), jnp.imag(freq)], 1)
        weighted = weight_two * plain
        per_band = jnp.dot(live_modes.T, weighted, precision=highest).reshape(BANDS, KMAX, 2 * BINS)
        projected = jnp.sum(per_band * mask_two[:, None, :], 0)
        block_sums = jnp.dot(members.T, weighted, precision=highest)
        mode_core = jnp.einsum("bkj,jf->bkf", core, projected, precision=highest) * mask_two[:, None, :]
        block_core = block_two * block_sums
        result = weight_two * (plain - jnp.dot(live_modes, mode_core.reshape(BANDS * KMAX, 2 * BINS), precision=highest) - jnp.dot(members, block_core, precision=highest))
        complex_bins = result[:, :BINS] + 1j * result[:, BINS:]
        complex_bins = jnp.concatenate([complex_bins, jnp.zeros((DETS, 1), complex_bins.dtype)], 1)
        return jnp.fft.irfft(complex_bins, n=SEGLEN, axis=1)[:, TAIL:]

    pieces = lax.map(one_segment, jnp.arange(seg_total, dtype=jnp.int32))
    return jnp.transpose(pieces, (1, 0, 2)).reshape(DETS, seg_total * STEP)
```

```python
import functools
import math

import jax
import jax.numpy as jnp
import numpy as np
from jax import lax
from jax.experimental import pallas as pl
from jax.experimental.pallas import tpu as pltpu
from jax.sharding import PartitionSpec as P

STEP = 256
TAIL = 256
BANDS = 8
KMAX = 16
NBLK = 16
SEGLEN = 512
BINS = 256
HALF = BINS // 2
MODES = BANDS * KMAX
COLS = BANDS * (KMAX + NBLK)
ROWS = KMAX + NBLK

F32 = jnp.float32
BF16 = jnp.bfloat16


def pieces_of(table):
    high = table.astype(BF16)
    low = (table - high.astype(np.float64)).astype(BF16)
    return jnp.asarray(high), jnp.asarray(low)


def make_tables():
    bins = np.concatenate([np.arange(0, BINS, 2), np.arange(1, BINS, 2)]).reshape(2, HALF)
    time = np.arange(STEP)
    angle = 2.0 * math.pi / SEGLEN * (time[:, None, None] * bins[None] % SEGLEN)
    forward = np.stack([np.cos(angle), -np.sin(angle)], 2).reshape(STEP, 2 * BINS)
    kept = np.arange(TAIL, SEGLEN)
    back = 2.0 * math.pi / SEGLEN * (bins[:, :, None] * kept % SEGLEN)
    factor = np.where(bins == 0, 1.0, 2.0)[:, :, None] / SEGLEN
    inverse = np.stack([factor * np.cos(back), -factor * np.sin(back)], 1).reshape(2 * BINS, STEP)
    return pieces_of(forward) + pieces_of(inverse)


def split(x):
    high = x.astype(BF16)
    return high, (x - high.astype(F32)).astype(BF16)


def dot(a, b):
    return jnp.dot(a, b, preferred_element_type=F32)


def dot3(a, b):
    return dot(a[0], b[0]) + (dot(a[0], b[1]) + dot(a[1], b[0]))


def band_rows(edges, width):
    col = lax.broadcasted_iota(jnp.int32, (1, width), 1)
    odd = (col >= width // 2).astype(jnp.int32)
    bin_idx = 2 * (col & (HALF - 1)) + odd
    return [
        ((bin_idx >= edges[b]) & (bin_idx < edges[b + 1])).astype(F32) for b in range(BANDS)
    ]


def project_kernel(
    counts, edges, x_ref, wt_ref, modes_ref, ids_ref, fh_ref, fl_ref, p_ref, v_ref, w_ref, acc
):
    step = pl.program_id(0)
    dets = x_ref.shape[0]
    wt = wt_ref[...]
    modes_t = modes_ref[...].T
    row = lax.broadcasted_iota(jnp.int32, (KMAX, dets), 0)
    mine = row == ids_ref[...]
    parts = []
    for b in range(BANDS):
        part = jnp.where(row < counts[b], modes_t[b * KMAX : (b + 1) * KMAX], 0.0)
        parts.append(part * wt[b : b + 1])
    for b in range(BANDS):
        parts.append(jnp.where(mine, wt[b : b + 1], 0.0))
    vt = jnp.concatenate(parts, 0)
    part = dot3(split(vt), split(x_ref[...]))

    @pl.when(step == 0)
    def _():
        acc[...] = part

    @pl.when(step > 0)
    def _():
        acc[...] += part

    high, low = split(vt.T)
    v_ref[:, :COLS] = high
    v_ref[:, COLS:] = low

    first = wt.astype(BF16).astype(F32)
    second = (wt - first).astype(BF16).astype(F32)
    third = wt - first - second
    stacked = jnp.concatenate([first, second, third], 0).T.astype(BF16)
    mask = jnp.concatenate(band_rows(edges, BINS), 0)
    w_ref[...] = dot(stacked, jnp.concatenate([mask] * 3, 0).astype(BF16))

    @pl.when(step == pl.num_programs(0) - 1)
    def _():
        masks = band_rows(edges, 2 * BINS)
        tables = fh_ref[...], fl_ref[...]
        for j in range(p_ref.shape[0]):
            g = dot3(split(acc[:, j * STEP : (j + 1) * STEP]), tables)
            for part_idx in range(2):
                total = 0.0
                for b in range(BANDS):
                    at = part_idx * MODES + b * KMAX
                    total += masks[b] * g[at : at + KMAX]
                p_ref[j, part_idx * KMAX : (part_idx + 1) * KMAX, :] = total


def filtered(early, late, w, tables):
    fh, fl, ih, il = tables
    even = dot3(split(early + late), (fh[:, :BINS], fl[:, :BINS]))
    odd = dot3(split(early - late), (fh[:, BINS:], fl[:, BINS:]))
    we, wo = w[:, :HALF], w[:, HALF:]
    weighted = jnp.concatenate(
        [even[:, :HALF] * we, even[:, HALF:] * we, odd[:, :HALF] * wo, odd[:, HALF:] * wo], 1
    )
    return dot3(split(weighted), (ih, il))


def main_kernel(x_ref, w_ref, fh_ref, fl_ref, ih_ref, il_ref, out_ref):
    tables = fh_ref[...], fl_ref[...], ih_ref[...], il_ref[...]
    x = x_ref[...]
    w = w_ref[...]
    for seg in range(1, x.shape[1] // STEP):
        early = x[:, (seg - 1) * STEP : seg * STEP]
        late = x[:, seg * STEP : (seg + 1) * STEP]
        out_ref[:, (seg - 1) * STEP : seg * STEP] = filtered(early, late, w, tables)


def correction(edges, before, after, core, coef, ih, il):
    masks = band_rows(edges, 2 * BINS)
    sums = jnp.concatenate(
        [before[:, :BINS] + after[:, :BINS], before[:, BINS:] - after[:, BINS:]], 1
    )
    mode_sums, block_sums = split(sums[:KMAX]), sums[KMAX:]
    core_h, core_l = split(core)
    mixed = dot(core_h, mode_sums[0]) + (dot(core_h, mode_sums[1]) + dot(core_l, mode_sums[0]))
    parts = [masks[b] * mixed[b * KMAX : (b + 1) * KMAX] for b in range(BANDS)]
    parts += [masks[b] * (coef[b * NBLK : (b + 1) * NBLK] * block_sums) for b in range(BANDS)]
    return split(dot3(split(jnp.concatenate(parts, 0)), (ih, il)))


def rest_kernel(edges, main_ref, p_ref, q_ref, v_ref, core_ref, coef_ref, ih_ref, il_ref, out_ref):
    seg = pl.program_id(0)
    z = correction(
        edges,
        p_ref[seg] + q_ref[seg],
        p_ref[seg + 1] + q_ref[seg + 1],
        core_ref[...],
        coef_ref[...],
        ih_ref[...],
        il_ref[...],
    )
    v = v_ref[...]
    out_ref[...] = main_ref[...] - dot3((v[:, :COLS], v[:, COLS:]), z)


def first_kernel(
    edges, tail_ref, x_ref, w_ref, v_ref, before_ref, p_ref, q_ref, core_ref, coef_ref,
    fh_ref, fl_ref, ih_ref, il_ref, _, out_ref, zh_ref, zl_ref,
):
    tables = fh_ref[...], fl_ref[...], ih_ref[...], il_ref[...]

    @pl.when(pl.program_id(0) == 0)
    def _():
        zh_ref[...], zl_ref[...] = correction(
            edges, before_ref[...], p_ref[...] + q_ref[...], core_ref[...], coef_ref[...], *tables[2:]
        )

    v = v_ref[...]
    z = zh_ref[...], zl_ref[...]
    main = filtered(tail_ref[...], x_ref[...], w_ref[...], tables)
    out_ref[...] = main - dot3((v[:, :COLS], v[:, COLS:]), z)


def whole(shape):
    return pl.BlockSpec(shape, lambda *_: (0,) * len(shape))


def cost(flops, nbytes):
    return pl.CostEstimate(flops=flops, bytes_accessed=nbytes, transcendentals=0)


def passed_along(block, axis, distance):
    devices = range(lax.axis_size(axis))
    route = [(i - distance, i) for i in devices if i - distance in devices]
    return lax.ppermute(block, axis, route)


def exchanged(block, axis, distance):
    devices = range(lax.axis_size(axis))
    return lax.ppermute(block, axis, [(i, i ^ distance) for i in devices])


def local(tod, inv_white, modes, mode_counts, core, block_coef, block_ids, band_edges):
    dets, samples = tod.shape
    segs = samples // STEP
    chunk = min(dets, 256)
    steps = dets // chunk
    fh, fl, ih, il = make_tables()
    table_specs = [whole(fh.shape), whole(fl.shape), whole(ih.shape), whole(il.shape)]
    core_rows = core.reshape(MODES, KMAX)
    coef_rows = block_coef.reshape(BANDS * NBLK, 1)

    before = passed_along(tod[:, samples - TAIL :], "tm", 1)

    sums, v, w = pl.pallas_call(
        project_kernel,
        out_shape=(
            jax.ShapeDtypeStruct((segs, ROWS, 2 * BINS), F32),
            jax.ShapeDtypeStruct((dets, 2 * COLS), BF16),
            jax.ShapeDtypeStruct((dets, BINS), F32),
        ),
        grid_spec=pltpu.PrefetchScalarGridSpec(
            num_scalar_prefetch=2,
            grid=(steps,),
            in_specs=[
                pl.BlockSpec((chunk, samples), lambda i, *_: (i, 0)),
                pl.BlockSpec((BANDS, chunk), lambda i, *_: (0, i)),
                pl.BlockSpec((chunk, MODES), lambda i, *_: (i, 0)),
                pl.BlockSpec((1, chunk), lambda i, *_: (0, i)),
                table_specs[0],
                table_specs[1],
            ],
            out_specs=(
                whole((segs, ROWS, 2 * BINS)),
                pl.BlockSpec((chunk, 2 * COLS), lambda i, *_: (i, 0)),
                pl.BlockSpec((chunk, BINS), lambda i, *_: (i, 0)),
            ),
            scratch_shapes=[pltpu.VMEM((COLS, samples), F32)],
        ),
        cost_estimate=cost(6 * dets * COLS * samples, 4 * dets * samples),
        name="project",
    )(mode_counts, band_edges, tod, inv_white.T, modes, block_ids.reshape(1, dets), fh, fl)

    main = pl.pallas_call(
        main_kernel,
        out_shape=jax.ShapeDtypeStruct((dets, samples - STEP), F32),
        grid=(steps,),
        in_specs=[
            pl.BlockSpec((chunk, samples), lambda i: (i, 0)),
            pl.BlockSpec((chunk, BINS), lambda i: (i, 0)),
            *table_specs,
        ],
        out_specs=pl.BlockSpec((chunk, samples - STEP), lambda i: (i, 0)),
        cost_estimate=cost(24 * dets * STEP * STEP * (segs - 1), 7 * dets * samples),
        name="main",
    )(tod, w, fh, fl, ih, il)

    distance = 1
    size = lax.axis_size("wafer")
    own, other = sums, jnp.zeros_like(sums)
    while distance < size:
        own = own + other if distance > 1 else own
        other = exchanged(own, "wafer", distance)
        distance *= 2
    last = own[segs - 1] + other[segs - 1]
    last_before = passed_along(last, "tm", 1)

    scalars = pltpu.PrefetchScalarGridSpec
    shared = [whole((MODES, KMAX)), whole((BANDS * NBLK, 1))]
    rest = pl.pallas_call(
        rest_kernel,
        out_shape=jax.ShapeDtypeStruct((dets, samples), F32),
        grid_spec=scalars(
            num_scalar_prefetch=1,
            grid=(segs - 1,),
            in_specs=[
                pl.BlockSpec((dets, STEP), lambda s, *_: (0, s)),
                whole(sums.shape),
                whole(sums.shape),
                whole(v.shape),
                *shared,
                *table_specs[2:],
            ],
            out_specs=pl.BlockSpec((dets, STEP), lambda s, *_: (0, s + 1)),
        ),
        cost_estimate=cost(6 * dets * COLS * STEP * (segs - 1), 8 * dets * samples),
        name="rest",
    )(band_edges, main, own, other, v, core_rows, coef_rows, ih, il)

    one = pl.BlockSpec((None, ROWS, 2 * BINS), lambda i, *_: (0, 0, 0))
    return pl.pallas_call(
        first_kernel,
        out_shape=jax.ShapeDtypeStruct((dets, samples), F32),
        grid_spec=scalars(
            num_scalar_prefetch=1,
            grid=(steps,),
            in_specs=[
                pl.BlockSpec((chunk, TAIL), lambda i, *_: (i, 0)),
                pl.BlockSpec((chunk, STEP), lambda i, *_: (i, 0)),
                pl.BlockSpec((chunk, BINS), lambda i, *_: (i, 0)),
                pl.BlockSpec((chunk, 2 * COLS), lambda i, *_: (i, 0)),
                whole(last.shape),
                one,
                one,
                *shared,
                *table_specs,
                pl.BlockSpec(memory_space=pl.ANY),
            ],
            out_specs=pl.BlockSpec((chunk, STEP), lambda i, *_: (i, 0)),
            scratch_shapes=[pltpu.VMEM((COLS, STEP), BF16)] * 2,
        ),
        input_output_aliases={14: 0},
        cost_estimate=cost(30 * dets * STEP * STEP, 12 * dets * STEP),
        name="first",
    )(band_edges, before, tod, w, v, last_before, own, other, core_rows, coef_rows, fh, fl, ih, il, rest)


def solution(mesh):
    return jax.shard_map(
        local,
        mesh=mesh,
        in_specs=(
            P(("real", "wafer"), "tm"),
            P("wafer", None),
            P("wafer", None),
            P(),
            P(),
            P(),
            P("wafer"),
            P(),
        ),
        out_specs=P(("real", "wafer"), "tm"),
        check_vma=False,
    )
```

```python
import math

import jax
import jax.numpy as jnp
import numpy as np
from jax import lax
from jax.experimental import pallas as pl
from jax.experimental.pallas import tpu as pltpu
from jax.sharding import PartitionSpec as P


STEP = 256
TAIL = 256
BANDS = 8
KMAX = 16
NBLK = 16
SEGLEN = 512
BINS = 256
HALF = BINS // 2
MODES = BANDS * KMAX
COLS = BANDS * (KMAX + NBLK)
ROWS = KMAX + NBLK

F32 = jnp.float32
BF16 = jnp.bfloat16


def pieces_of(table):
    high = table.astype(BF16)
    low = (table - high.astype(np.float64)).astype(BF16)
    return jnp.asarray(high), jnp.asarray(low)


def make_tables():
    bins = np.concatenate([np.arange(0, BINS, 2), np.arange(1, BINS, 2)]).reshape(2, HALF)
    time = np.arange(STEP)
    angle = 2.0 * math.pi / SEGLEN * (time[:, None, None] * bins[None] % SEGLEN)
    forward = np.stack([np.cos(angle), -np.sin(angle)], 2).reshape(STEP, 2 * BINS)
    kept = np.arange(TAIL, SEGLEN)
    back = 2.0 * math.pi / SEGLEN * (bins[:, :, None] * kept % SEGLEN)
    factor = np.where(bins == 0, 1.0, 2.0)[:, :, None] / SEGLEN
    inverse = np.stack([factor * np.cos(back), -factor * np.sin(back)], 1).reshape(2 * BINS, STEP)
    return pieces_of(forward) + pieces_of(inverse)


def split(x):
    high = x.astype(BF16)
    return high, (x - high.astype(F32)).astype(BF16)


def three(x):
    first = x.astype(BF16).astype(F32)
    second = (x - first).astype(BF16).astype(F32)
    return jnp.concatenate([first, second, x - first - second], 0).astype(BF16)


def dot(a, b):
    return jnp.dot(a, b, preferred_element_type=F32)


def dot3(a, b):
    return dot(a[0], b[0]) + (dot(a[0], b[1]) + dot(a[1], b[0]))


def band_rows(edges, width):
    col = lax.broadcasted_iota(jnp.int32, (1, width), 1)
    odd = (col >= width // 2).astype(jnp.int32)
    bin_idx = 2 * (col & (HALF - 1)) + odd
    return [
        ((bin_idx >= edges[b]) & (bin_idx < edges[b + 1])).astype(F32) for b in range(BANDS)
    ]


def chunk_of(count, most):
    return most if count % most == 0 else count


def rows_of(ref, most=256):
    count = ref.shape[0]
    size = chunk_of(count, most)
    return [slice(start, start + size) for start in range(0, count, size)]


def started(copies):
    for copy in copies:
        copy.start()
    return copies


def waited(copies):
    for copy in copies:
        copy.wait()


def tail_kernel(tod_ref, out_ref, sem):
    first = tod_ref.shape[1] - out_ref.shape[1]
    waited(
        started(
            [
                pltpu.make_async_copy(tod_ref.at[here, first:], out_ref.at[here, :], sem.at[i])
                for i, here in enumerate(rows_of(out_ref))
            ]
        )
    )


def project_kernel(
    counts, edges, tod_ref, wt_hbm, modes_hbm, ids_hbm, fh_hbm, fl_hbm, ih_hbm, il_hbm, tail_ref,
    p_ref, v_ref, w_ref, x_ref, fh_ref, fl_ref, ih_ref, il_ref, wt_ref, modes_ref, ids_ref, sem,
):
    dets, known = x_ref.shape
    segs = p_ref.shape[0]
    chunks = rows_of(x_ref)
    chunk = dets // len(chunks)
    moves = [(wt_hbm, wt_ref), (ids_hbm, ids_ref), (modes_hbm, modes_ref)]
    moves += [(tod_ref.at[here, :known], x_ref.at[here, :]) for here in chunks]
    moves += [(fh_hbm, fh_ref), (fl_hbm, fl_ref), (ih_hbm, ih_ref), (il_hbm, il_ref)]
    copies = started(
        [pltpu.make_async_copy(a, b, sem.at[i]) for i, (a, b) in enumerate(moves)]
    )
    mask = jnp.concatenate(band_rows(edges, BINS), 0)
    mask = jnp.concatenate([mask] * 3, 0).astype(BF16)
    row = lax.broadcasted_iota(jnp.int32, (KMAX, chunk), 0)
    waited(copies[:3])
    vts = []
    for here in chunks:
        wt = wt_ref[:, here]
        modes_t = modes_ref[here, :].T
        mine = row == ids_ref[:, here]
        parts = []
        for b in range(BANDS):
            part = jnp.where(row < counts[b], modes_t[b * KMAX : (b + 1) * KMAX], 0.0)
            parts.append(part * wt[b : b + 1])
        for b in range(BANDS):
            parts.append(jnp.where(mine, wt[b : b + 1], 0.0))
        vt = jnp.concatenate(parts, 0)
        v_ref[here, :COLS], v_ref[here, COLS:] = split(vt.T)
        vts.append(vt)
        w_ref[here, :] = lax.dot_general(
            three(wt), mask, (((0,), (0,)), ((), ())), preferred_element_type=F32
        )
    waited(copies[3:])
    vt = split(jnp.concatenate(vts, 1))
    q = [dot3(vt, split(x_ref[:, at : at + STEP])) for at in range(0, known, STEP)]
    q = jnp.concatenate(q + [dot3(vt, split(tail_ref[...]))], 0)
    g = dot3(split(q), (fh_ref[...], fl_ref[...]))
    masks = band_rows(edges, 2 * BINS)
    for j in range(segs):
        for part_idx in range(2):
            total = 0.0
            for b in range(BANDS):
                at = j * COLS + part_idx * MODES + b * KMAX
                total += masks[b] * g[at : at + KMAX]
            p_ref[j, part_idx * KMAX : (part_idx + 1) * KMAX, :] = total


def filtered(pairs, w, tables):
    fh, fl, ih, il = tables
    sums = split(jnp.concatenate([early + late for early, late in pairs], 0))
    gaps = split(jnp.concatenate([early - late for early, late in pairs], 0))
    even = dot3(sums, (fh[:, :BINS], fl[:, :BINS]))
    odd = dot3(gaps, (fh[:, BINS:], fl[:, BINS:]))
    we = jnp.concatenate([jnp.concatenate([w[:, :HALF]] * 2, 1)] * len(pairs), 0)
    wo = jnp.concatenate([jnp.concatenate([w[:, HALF:]] * 2, 1)] * len(pairs), 0)
    return dot3(split(even * we), (ih[:BINS], il[:BINS])) + dot3(
        split(odd * wo), (ih[BINS:], il[BINS:])
    )


def main_kernel(x_ref, tail_ref, w_ref, fh_ref, fl_ref, ih_ref, il_ref, out_ref):
    tables = fh_ref[...], fl_ref[...], ih_ref[...], il_ref[...]
    known = x_ref.shape[1]
    for here in rows_of(x_ref, 512):
        blocks = [x_ref[here, at : at + STEP] for at in range(0, known, STEP)]
        blocks.append(tail_ref[here, :])
        y = filtered(list(zip(blocks, blocks[1:])), w_ref[here, :], tables)
        chunk = here.stop - here.start
        for seg in range(len(blocks) - 1):
            out_ref[here, seg * STEP : (seg + 1) * STEP] = y[seg * chunk : (seg + 1) * chunk]


def to_correct(edges, before, after, core, coef):
    masks = band_rows(edges, 2 * BINS)
    sums = jnp.concatenate(
        [before[:, :BINS] + after[:, :BINS], before[:, BINS:] - after[:, BINS:]], 1
    )
    core = jnp.concatenate([core[b] for b in range(BANDS)], 0)
    mixed = dot3(split(core), split(sums[:KMAX]))
    mask = jnp.concatenate(masks * 3, 0).astype(BF16)
    levels = lax.dot_general(
        three(coef), mask, (((0,), (0,)), ((), ())), preferred_element_type=F32
    )
    blocks = levels * sums[KMAX:]
    parts = [masks[b] * mixed[b * KMAX : (b + 1) * KMAX] for b in range(BANDS)]
    return jnp.concatenate(parts + [masks[b] * blocks for b in range(BANDS)], 0)


def rest_kernel(
    edges, core_hbm, coef_hbm, main_ref, p_ref, q_ref, v_ref, ih_ref, il_ref,
    out_ref, core_ref, coef_ref, buf, sem,
):
    segs = p_ref.shape[0]
    waited(
        started(
            [
                pltpu.make_async_copy(core_hbm, core_ref, sem.at[0]),
                pltpu.make_async_copy(coef_hbm, coef_ref, sem.at[1]),
            ]
        )
    )
    sums = [p_ref[j] + q_ref[j] for j in range(segs)]
    core, coef = core_ref[...], coef_ref[...]
    rows = [to_correct(edges, a, b, core, coef) for a, b in zip(sums, sums[1:])]
    z = dot3(split(jnp.concatenate(rows, 0)), (ih_ref[...], il_ref[...]))
    z = split(jnp.concatenate([z[g * COLS : (g + 1) * COLS] for g in range(segs - 1)], 1))
    copies = []
    for i, here in enumerate(rows_of(buf)):
        buf[here, :] = main_ref[here, :] - dot3((v_ref[here, :COLS], v_ref[here, COLS:]), z)
        copies += started(
            [pltpu.make_async_copy(buf.at[here, :], out_ref.at[here, STEP:], sem.at[2 + i])]
        )
    waited(copies)


def first_kernel(
    edges, core_hbm, coef_hbm, tod_ref, _, odd_ref, even_ref, w_ref, v_ref, before_ref, p_ref,
    q_ref, fh_ref, fl_ref, ih_ref, il_ref, out_ref, core_ref, coef_ref, x_ref, buf, sem,
):
    tables = fh_ref[...], fl_ref[...], ih_ref[...], il_ref[...]
    place = lax.axis_index("tm")
    follows = place > 0
    here_odd = place % 2 == 1
    chunks = rows_of(buf)

    late_copy = pltpu.make_async_copy(tod_ref.at[:, :STEP], x_ref, sem.at[2 + len(chunks)])
    late_copy.start()
    waited(
        started(
            [
                pltpu.make_async_copy(core_hbm, core_ref, sem.at[0]),
                pltpu.make_async_copy(coef_hbm, coef_ref, sem.at[1]),
            ]
        )
    )
    before = jnp.where(follows, before_ref[...], 0.0)
    rows = to_correct(edges, before, p_ref[0] + q_ref[0], core_ref[...], coef_ref[...])
    z = split(dot3(split(rows), tables[2:]))
    late_copy.wait()
    copies = []
    for i, here in enumerate(chunks):
        tail = jnp.where(here_odd, odd_ref[here, :], even_ref[here, :])
        tail = jnp.where(follows, tail, 0.0)
        y = filtered([(tail, x_ref[here, :])], w_ref[here, :], tables)
        buf[here, :] = y - dot3((v_ref[here, :COLS], v_ref[here, COLS:]), z)
        copies += started(
            [pltpu.make_async_copy(buf.at[here, :], out_ref.at[here, :STEP], sem.at[2 + i])]
        )
    waited(copies)


IN_VMEM = pl.BlockSpec(memory_space=pltpu.VMEM)
ANYWHERE = pl.BlockSpec(memory_space=pl.ANY)


def run(kernel, scalars, loose, kept, outs, scratch=(), alias=None, flops=0, nbytes=0, mib=24):
    loose = [pltpu.with_memory_space_constraint(a, pltpu.HBM) for a in loose]
    kept = [pltpu.with_memory_space_constraint(a, pltpu.VMEM) for a in kept]
    many = isinstance(outs, tuple)
    places = tuple(
        ANYWHERE if isinstance(o, jax.ShapeDtypeStruct) else IN_VMEM for o in (outs if many else (outs,))
    )
    return pl.pallas_call(
        kernel,
        out_shape=outs,
        grid_spec=pltpu.PrefetchScalarGridSpec(
            num_scalar_prefetch=len(scalars),
            grid=(),
            in_specs=[ANYWHERE] * len(loose) + [IN_VMEM] * len(kept),
            out_specs=places if many else places[0],
            scratch_shapes=list(scratch),
        ),
        input_output_aliases=alias or {},
        cost_estimate=pl.CostEstimate(flops=flops, bytes_accessed=nbytes, transcendentals=0),
        compiler_params=pltpu.CompilerParams(vmem_limit_bytes=mib << 20),
    )(*scalars, *loose, *kept)


def exchanged(block, axis, distance):
    devices = range(lax.axis_size(axis))
    return lax.ppermute(block, axis, [(i, i ^ distance) for i in devices])


def pair_swap(block, parity):
    n, m = lax.axis_size("tm"), lax.axis_size("wafer")
    route = []
    for t in range(n):
        mate = t + 1 if t % 2 == parity else t - 1
        for w in range(m):
            near = w ^ 1 if w ^ 1 < m else w
            to = (mate, w) if 0 <= mate < n else (t, near)
            route.append((t * m + w, to[0] * m + to[1]))
    return lax.ppermute(block, ("tm", "wafer"), route)


def local(tod, inv_white, modes, mode_counts, core, block_coef, block_ids, band_edges):
    dets, samples = tod.shape
    segs = samples // STEP
    known = samples - TAIL
    tables = make_tables()
    along = lax.axis_size("tm")
    count = dets // chunk_of(dets, 256)
    whole = jax.ShapeDtypeStruct((dets, samples), F32)
    small = [pltpu.VMEM(core.shape, F32), pltpu.VMEM((BANDS, NBLK), F32)]

    tail = run(
        tail_kernel,
        (),
        (tod,),
        (),
        pltpu.VMEM((dets, TAIL), F32),
        scratch=[pltpu.SemaphoreType.DMA((count,))],
        nbytes=8 * dets * TAIL,
    )
    odd = pair_swap(tail, 0)
    even = pair_swap(tail, 1)

    sums, v, w, x, *tables = run(
        project_kernel,
        (mode_counts, band_edges),
        (tod, inv_white.T, modes, block_ids.reshape(1, dets), *tables),
        (tail,),
        (
            pltpu.VMEM((segs, ROWS, 2 * BINS), F32),
            pltpu.VMEM((dets, 2 * COLS), BF16),
            pltpu.VMEM((dets, BINS), F32),
            pltpu.VMEM((dets, known), F32),
            *[pltpu.VMEM(t.shape, BF16) for t in tables],
        ),
        scratch=[
            pltpu.VMEM((BANDS, dets), F32),
            pltpu.VMEM((dets, MODES), F32),
            pltpu.VMEM((1, dets), jnp.int32),
            pltpu.SemaphoreType.DMA((count + 7,)),
        ],
        flops=6 * dets * COLS * samples,
        nbytes=4 * dets * samples,
    )
    main = run(
        main_kernel,
        (),
        (),
        (x, tail, w, *tables),
        pltpu.VMEM((dets, known), F32),
        flops=24 * dets * STEP * known,
        nbytes=7 * dets * samples,
    )

    own, other, distance = sums, jnp.zeros_like(sums), 1
    while distance < lax.axis_size("wafer"):
        own = own + other if distance > 1 else own
        other = exchanged(own, "wafer", distance)
        distance *= 2
    last = own[segs - 1] + other[segs - 1]
    before = lax.ppermute(last, "tm", [(i, (i + 1) % along) for i in range(along)])

    rest = run(
        rest_kernel,
        (band_edges,),
        (core, block_coef),
        (main, own, other, v, *tables[2:]),
        whole,
        scratch=[
            *small,
            pltpu.VMEM((dets, known), F32),
            pltpu.SemaphoreType.DMA((count + 2,)),
        ],
        flops=6 * dets * COLS * known,
        nbytes=4 * dets * samples,
    )
    return run(
        first_kernel,
        (band_edges,),
        (core, block_coef, tod, rest),
        (odd, even, w, v, before, own, other, *tables),
        whole,
        scratch=[
            *small,
            pltpu.VMEM((dets, STEP), F32),
            pltpu.VMEM((dets, STEP), F32),
            pltpu.SemaphoreType.DMA((count + 3,)),
        ],
        alias={4: 0},
        flops=30 * dets * STEP * STEP,
        nbytes=4 * dets * STEP,
    )


def solution(mesh):
    return jax.shard_map(
        local,
        mesh=mesh,
        in_specs=(
            P(("real", "wafer"), "tm"),
            P("wafer", None),
            P("wafer", None),
            P(),
            P(),
            P(),
            P("wafer"),
            P(),
        ),
        out_specs=P(("real", "wafer"), "tm"),
        check_vma=False,
    )
```

```python
import math

import jax
import jax.numpy as jnp
import numpy as np
from jax import lax
from jax.experimental import pallas as pl
from jax.experimental.pallas import tpu as pltpu
from jax.sharding import PartitionSpec as P


STEP = 256
TAIL = 256
BANDS = 8
KMAX = 16
NBLK = 16
SEGLEN = 512
BINS = 256
HALF = BINS // 2
MODES = BANDS * KMAX
COLS = BANDS * (KMAX + NBLK)
ROWS = KMAX + NBLK

F32 = jnp.float32
BF16 = jnp.bfloat16


def pieces_of(table):
    high = table.astype(BF16)
    low = (table - high.astype(np.float64)).astype(BF16)
    return jnp.asarray(high), jnp.asarray(low)


def make_tables():
    bins = np.concatenate([np.arange(0, BINS, 2), np.arange(1, BINS, 2)]).reshape(2, HALF)
    time = np.arange(STEP)
    angle = 2.0 * math.pi / SEGLEN * (time[:, None, None] * bins[None] % SEGLEN)
    forward = np.stack([np.cos(angle), -np.sin(angle)], 2).reshape(STEP, 2 * BINS)
    kept = np.arange(TAIL, SEGLEN)
    back = 2.0 * math.pi / SEGLEN * (bins[:, :, None] * kept % SEGLEN)
    factor = np.where(bins == 0, 1.0, 2.0)[:, :, None] / SEGLEN
    inverse = np.stack([factor * np.cos(back), -factor * np.sin(back)], 1).reshape(2 * BINS, STEP)
    return pieces_of(forward) + pieces_of(inverse)


def split(x):
    high = x.astype(BF16)
    return high, (x - high.astype(F32)).astype(BF16)


def three(x):
    first = x.astype(BF16).astype(F32)
    second = (x - first).astype(BF16).astype(F32)
    return jnp.concatenate([first, second, x - first - second], 0).astype(BF16)


def dot(a, b):
    return jnp.dot(a, b, preferred_element_type=F32)


def dot3(a, b):
    return dot(a[0], b[0]) + (dot(a[0], b[1]) + dot(a[1], b[0]))


def band_rows(edges, width):
    col = lax.broadcasted_iota(jnp.int32, (1, width), 1)
    odd = (col >= width // 2).astype(jnp.int32)
    bin_idx = 2 * (col & (HALF - 1)) + odd
    rows = [
        (bin_idx >= edges[:, b : b + 1]) & (bin_idx < edges[:, b + 1 : b + 2])
        for b in range(BANDS)
    ]
    return jnp.concatenate([row.astype(F32) for row in rows], 0)


def chunk_of(count, most):
    return most if count % most == 0 else count


def rows_of(ref, most=256):
    count = ref.shape[0]
    size = chunk_of(count, most)
    return [slice(start, start + size) for start in range(0, count, size)]


def started(copies):
    for copy in copies:
        copy.start()
    return copies


def waited(copies):
    for copy in copies:
        copy.wait()


def load_kernel(tod_ref, *refs):
    count = (len(refs) - 3) // 2
    small, (soon_ref, late_ref), kept, sem = refs[:count], refs[count : count + 2], refs[count + 2 : -1], refs[-1]
    first = tod_ref.shape[1] - TAIL
    moves, done = [], 0
    for part in (soon_ref, late_ref):
        for here in rows_of(part):
            there = slice(done + here.start, done + here.stop)
            moves.append((tod_ref.at[there, first:], part.at[here, :]))
        done += part.shape[0]
    moves += list(zip(small, kept))
    waited(
        started([pltpu.make_async_copy(a, b, sem.at[i]) for i, (a, b) in enumerate(moves)])
    )


def project_kernel(
    tod_ref, wt_ref, modes_ref, ids_ref, counts_ref, edges_ref, fh_ref, fl_ref,
    p_ref, vt_ref, mask_ref,
):
    segs = p_ref.shape[0]
    counts = counts_ref[...]
    mask = band_rows(edges_ref[...], 2 * BINS)
    mask_ref[...] = mask
    vts = []
    for here in rows_of(modes_ref):
        wt = wt_ref[:, here]
        modes_t = modes_ref[here, :].T
        row = lax.broadcasted_iota(jnp.int32, (KMAX, here.stop - here.start), 0)
        mine = row == ids_ref[:, here]
        parts = []
        for b in range(BANDS):
            part = jnp.where(row < counts[:, b : b + 1], modes_t[b * KMAX : (b + 1) * KMAX], 0.0)
            parts.append(part * wt[b : b + 1])
        for b in range(BANDS):
            parts.append(jnp.where(mine, wt[b : b + 1], 0.0))
        vts.append(jnp.concatenate(parts, 0))
        vt_ref[:, here] = vts[-1]
    vt = split(jnp.concatenate(vts, 1))
    q = [dot3(vt, split(tod_ref[:, j * STEP : (j + 1) * STEP])) for j in range(segs)]
    g = dot3(split(jnp.concatenate(q, 0)), (fh_ref[...], fl_ref[...]))
    for j in range(segs):
        for part_idx in range(2):
            total = 0.0
            for b in range(BANDS):
                at = j * COLS + part_idx * MODES + b * KMAX
                total += mask[b : b + 1] * g[at : at + KMAX]
            p_ref[j, part_idx * KMAX : (part_idx + 1) * KMAX, :] = total


def prepare_kernel(vt_ref, wt_ref, mask_ref, coef_ref, v_ref, w_ref, levels_ref):
    mask = jnp.concatenate([mask_ref[...]] * 3, 0).astype(BF16)
    across = (((0,), (0,)), ((), ()))
    levels_ref[...] = lax.dot_general(
        three(coef_ref[...]), mask, across, preferred_element_type=F32
    )
    one_each = jnp.concatenate([mask[:, :HALF], mask[:, BINS : BINS + HALF]], 1)
    for here in rows_of(v_ref):
        v_ref[here, :COLS], v_ref[here, COLS:] = split(vt_ref[:, here].T)
        w_ref[here, :] = lax.dot_general(
            three(wt_ref[:, here]), one_each, across, preferred_element_type=F32
        )


def filtered(pairs, w, tables):
    fh, fl, ih, il = tables
    sums = split(jnp.concatenate([early + late for early, late in pairs], 0))
    gaps = split(jnp.concatenate([early - late for early, late in pairs], 0))
    even = dot3(sums, (fh[:, :BINS], fl[:, :BINS]))
    odd = dot3(gaps, (fh[:, BINS:], fl[:, BINS:]))
    we = jnp.concatenate([jnp.concatenate([w[:, :HALF]] * 2, 1)] * len(pairs), 0)
    wo = jnp.concatenate([jnp.concatenate([w[:, HALF:]] * 2, 1)] * len(pairs), 0)
    return dot3(split(even * we), (ih[:BINS], il[:BINS])) + dot3(
        split(odd * wo), (ih[BINS:], il[BINS:])
    )


def main_kernel(tod_ref, w_ref, fh_ref, fl_ref, ih_ref, il_ref, out_ref):
    tables = fh_ref[...], fl_ref[...], ih_ref[...], il_ref[...]
    for here in rows_of(tod_ref, 512):
        blocks = [tod_ref[here, at : at + STEP] for at in range(0, tod_ref.shape[1], STEP)]
        y = filtered(list(zip(blocks, blocks[1:])), w_ref[here, :], tables)
        chunk = here.stop - here.start
        for seg in range(len(blocks) - 1):
            out_ref[here, seg * STEP : (seg + 1) * STEP] = y[seg * chunk : (seg + 1) * chunk]


def pack_kernel(late_ref, p_ref, q_ref, out_ref):
    late = late_ref.shape[0]
    out_ref[:late, :] = late_ref[...]
    sums = p_ref[p_ref.shape[0] - 1] + q_ref[q_ref.shape[0] - 1]
    out_ref[late : late + ROWS, :] = sums[:, :BINS]
    out_ref[late + ROWS :, :] = sums[:, BINS:]


def to_correct(mask, before, after, core, levels):
    sums = jnp.concatenate(
        [before[:, :BINS] + after[:, :BINS], before[:, BINS:] - after[:, BINS:]], 1
    )
    core = jnp.concatenate([core[b] for b in range(BANDS)], 0)
    mixed = dot3(split(core), split(sums[:KMAX]))
    blocks = levels * sums[KMAX:]
    masks = [mask[b : b + 1] for b in range(BANDS)]
    parts = [masks[b] * mixed[b * KMAX : (b + 1) * KMAX] for b in range(BANDS)]
    return jnp.concatenate(parts + [masks[b] * blocks for b in range(BANDS)], 0)


def rest_kernel(
    main_ref, p_ref, q_ref, v_ref, mask_ref, levels_ref, core_ref, ih_ref, il_ref,
    out_ref, buf, sem,
):
    segs = p_ref.shape[0]
    sums = [p_ref[j] + q_ref[j] for j in range(segs)]
    mask, levels, core = mask_ref[...], levels_ref[...], core_ref[...]
    rows = [to_correct(mask, a, b, core, levels) for a, b in zip(sums, sums[1:])]
    z = dot3(split(jnp.concatenate(rows, 0)), (ih_ref[...], il_ref[...]))
    z = split(jnp.concatenate([z[g * COLS : (g + 1) * COLS] for g in range(segs - 1)], 1))
    copies = []
    for i, here in enumerate(rows_of(buf)):
        buf[here, :] = main_ref[here, :] - dot3((v_ref[here, :COLS], v_ref[here, COLS:]), z)
        copies += started(
            [pltpu.make_async_copy(buf.at[here, :], out_ref.at[here, STEP:], sem.at[i])]
        )
    waited(copies)


def came(odd_ref, even_ref, here):
    place = lax.axis_index("tm")
    sent = jnp.where(place % 2 == 1, odd_ref[here, :], even_ref[here, :])
    return jnp.where(place > 0, sent, 0.0)


def soon_kernel(odd_ref, even_ref, tod_ref, w_ref, fh_ref, fl_ref, ih_ref, il_ref, out_ref):
    tables = fh_ref[...], fl_ref[...], ih_ref[...], il_ref[...]
    for here in rows_of(out_ref, out_ref.shape[0]):
        pair = came(odd_ref, even_ref, here), tod_ref[here, :STEP]
        out_ref[here, :] = filtered([pair], w_ref[here, :], tables)


def late_kernel(
    _, soon_ref, odd_ref, even_ref, tod_ref, w_ref, p_ref, q_ref, v_ref, mask_ref, levels_ref,
    core_ref, fh_ref, fl_ref, ih_ref, il_ref, out_ref, buf, sem,
):
    tables = fh_ref[...], fl_ref[...], ih_ref[...], il_ref[...]
    soon = soon_ref.shape[0]
    late = buf.shape[0] - soon
    before = came(odd_ref, even_ref, slice(late, late + 2 * ROWS))
    before = jnp.concatenate([before[:ROWS], before[ROWS:]], 1)
    rows = to_correct(
        mask_ref[...], before, p_ref[0] + q_ref[0], core_ref[...], levels_ref[...]
    )
    z = split(dot3(split(rows), tables[2:]))
    here = slice(soon, soon + late)
    pair = came(odd_ref, even_ref, slice(0, late)), tod_ref[here, :STEP]
    last = filtered([pair], w_ref[here, :], tables)
    copies = []
    for i, here in enumerate(rows_of(soon_ref, late * 2) + [here]):
        y = last if here.start == soon else soon_ref[here, :]
        buf[here, :] = y - dot3((v_ref[here, :COLS], v_ref[here, COLS:]), z)
        copies += started(
            [pltpu.make_async_copy(buf.at[here, :], out_ref.at[here, :STEP], sem.at[i])]
        )
    waited(copies)


IN_VMEM = pl.BlockSpec(memory_space=pltpu.VMEM)
ANYWHERE = pl.BlockSpec(memory_space=pl.ANY)


def run(kernel, loose, kept, outs, scratch=(), alias=None, flops=0, nbytes=0):
    loose = [pltpu.with_memory_space_constraint(a, pltpu.HBM) for a in loose]
    kept = [pltpu.with_memory_space_constraint(a, pltpu.VMEM) for a in kept]
    many = isinstance(outs, tuple)
    places = tuple(
        ANYWHERE if isinstance(o, jax.ShapeDtypeStruct) else IN_VMEM for o in (outs if many else (outs,))
    )
    return pl.pallas_call(
        kernel,
        out_shape=outs,
        in_specs=[ANYWHERE] * len(loose) + [IN_VMEM] * len(kept),
        out_specs=places if many else places[0],
        scratch_shapes=list(scratch),
        input_output_aliases=alias or {},
        cost_estimate=pl.CostEstimate(flops=flops, bytes_accessed=nbytes, transcendentals=0),
        compiler_params=pltpu.CompilerParams(vmem_limit_bytes=24 << 20),
    )(*loose, *kept)


def exchanged(block, axis, distance):
    devices = range(lax.axis_size(axis))
    return lax.ppermute(block, axis, [(i, i ^ distance) for i in devices])


def pair_swap(block, parity):
    n, m = lax.axis_size("tm"), lax.axis_size("wafer")
    route = []
    for t in range(n):
        mate = t + 1 if t % 2 == parity else t - 1
        for w in range(m):
            near = w ^ 1 if w ^ 1 < m else w
            to = (mate, w) if 0 <= mate < n else (t, near)
            route.append((t * m + w, to[0] * m + to[1]))
    return lax.ppermute(block, ("tm", "wafer"), route)


def local(tod, inv_white, modes, mode_counts, core, block_coef, block_ids, band_edges):
    dets, samples = tod.shape
    segs = samples // STEP
    known = samples - TAIL
    fh, fl, ih, il = tables = make_tables()
    late = dets // 8
    soon = dets - late
    whole = jax.ShapeDtypeStruct((dets, samples), F32)

    small = (
        inv_white.T,
        modes,
        block_ids.reshape(1, dets),
        mode_counts.reshape(1, BANDS),
        band_edges.reshape(1, BANDS + 1),
    )
    tail, late_tail, wt, *small = run(
        load_kernel,
        (tod, *small),
        (),
        (
            pltpu.VMEM((soon, TAIL), F32),
            pltpu.VMEM((late, TAIL), F32),
            *[pltpu.VMEM(a.shape, a.dtype) for a in small],
        ),
        scratch=[pltpu.SemaphoreType.DMA((dets // late + 8,))],
        nbytes=8 * dets * TAIL,
    )
    odd_soon = pair_swap(tail, 0)
    even_soon = pair_swap(tail, 1)

    sums, vt, mask = run(
        project_kernel,
        (),
        (tod, wt, *small, fh, fl),
        (
            pltpu.VMEM((segs, ROWS, 2 * BINS), F32),
            pltpu.VMEM((COLS, dets), F32),
            pltpu.VMEM((BANDS, 2 * BINS), F32),
        ),
        flops=6 * dets * COLS * samples,
        nbytes=4 * dets * samples,
    )
    v, w, levels = run(
        prepare_kernel,
        (),
        (vt, wt, mask, block_coef),
        (
            pltpu.VMEM((dets, 2 * COLS), BF16),
            pltpu.VMEM((dets, BINS), F32),
            pltpu.VMEM((NBLK, 2 * BINS), F32),
        ),
        flops=6 * dets * COLS * BANDS,
        nbytes=8 * dets * COLS,
    )
    main = run(
        main_kernel,
        (),
        (tod, w, *tables),
        pltpu.VMEM((dets, known), F32),
        flops=24 * dets * STEP * known,
        nbytes=7 * dets * samples,
    )

    own, other, distance = sums, jnp.zeros_like(sums), 1
    while distance < lax.axis_size("wafer"):
        own = own + other if distance > 1 else own
        other = exchanged(own, "wafer", distance)
        distance *= 2

    packed = run(
        pack_kernel,
        (),
        (late_tail, own, other),
        pltpu.VMEM((late + 2 * ROWS, TAIL), F32),
        nbytes=8 * late * TAIL,
    )
    odd_late = pair_swap(packed, 0)
    even_late = pair_swap(packed, 1)

    rest = run(
        rest_kernel,
        (),
        (main, own, other, v, mask, levels, core, ih, il),
        whole,
        scratch=[pltpu.VMEM((dets, known), F32), pltpu.SemaphoreType.DMA((16,))],
        flops=6 * dets * COLS * known,
        nbytes=4 * dets * samples,
    )
    filtered_soon = run(
        soon_kernel,
        (),
        (odd_soon, even_soon, tod, w, *tables),
        pltpu.VMEM((soon, STEP), F32),
        flops=24 * soon * STEP * STEP,
        nbytes=8 * soon * STEP,
    )
    return run(
        late_kernel,
        (rest,),
        (filtered_soon, odd_late, even_late, tod, w, own, other, v, mask, levels, core, *tables),
        whole,
        scratch=[pltpu.VMEM((dets, STEP), F32), pltpu.SemaphoreType.DMA((16,))],
        alias={0: 0},
        flops=6 * dets * STEP * STEP,
        nbytes=4 * dets * STEP,
    )


def solution(mesh):
    return jax.shard_map(
        local,
        mesh=mesh,
        in_specs=(
            P(("real", "wafer"), "tm"),
            P("wafer", None),
            P("wafer", None),
            P(),
            P(),
            P(),
            P("wafer"),
            P(),
        ),
        out_specs=P(("real", "wafer"), "tm"),
        check_vma=False,
    )
```

```python
import math

import jax
import jax.numpy as jnp
import numpy as np
from jax import lax
from jax.experimental import pallas as pl
from jax.experimental.pallas import tpu as pltpu
from jax.sharding import PartitionSpec as P


STEP = 256
TAIL = 256
BANDS = 8
KMAX = 16
NBLK = 16
SEGLEN = 512
BINS = 256
HALF = BINS // 2
MODES = BANDS * KMAX
COLS = BANDS * (KMAX + NBLK)
ROWS = KMAX + NBLK


F32 = jnp.float32
BF16 = jnp.bfloat16


def pieces_of(table):
    high = table.astype(BF16)
    low = (table - high.astype(np.float64)).astype(BF16)
    return jnp.asarray(high), jnp.asarray(low)


def make_tables():
    bins = np.concatenate([np.arange(0, BINS, 2), np.arange(1, BINS, 2)]).reshape(2, HALF)
    time = np.arange(STEP)
    angle = 2.0 * math.pi / SEGLEN * (time[:, None, None] * bins[None] % SEGLEN)
    forward = np.stack([np.cos(angle), -np.sin(angle)], 2).reshape(STEP, 2 * BINS)
    kept = np.arange(TAIL, SEGLEN)
    back = 2.0 * math.pi / SEGLEN * (bins[:, :, None] * kept % SEGLEN)
    factor = np.where(bins == 0, 1.0, 2.0)[:, :, None] / SEGLEN
    inverse = np.stack([factor * np.cos(back), -factor * np.sin(back)], 1).reshape(2 * BINS, STEP)
    return pieces_of(forward) + pieces_of(inverse)


def split(x):
    high = x.astype(BF16)
    return high, (x - high.astype(F32)).astype(BF16)


def three(x):
    first = x.astype(BF16).astype(F32)
    second = (x - first).astype(BF16).astype(F32)
    return jnp.concatenate([first, second, x - first - second], 0).astype(BF16)


def dot(a, b):
    return jnp.dot(a, b, preferred_element_type=F32)


def dot3(a, b):
    return dot(a[0], b[0]) + (dot(a[0], b[1]) + dot(a[1], b[0]))


def band_rows(edges, width):
    col = lax.broadcasted_iota(jnp.int32, (1, width), 1)
    odd = (col >= width // 2).astype(jnp.int32)
    bin_idx = 2 * (col & (HALF - 1)) + odd
    rows = [
        (bin_idx >= edges[:, b : b + 1]) & (bin_idx < edges[:, b + 1 : b + 2])
        for b in range(BANDS)
    ]
    return jnp.concatenate([row.astype(F32) for row in rows], 0)


def chunk_of(count, most):
    return most if count % most == 0 else count


def rows_of(ref, most=256):
    count = ref.shape[0]
    size = chunk_of(count, most)
    return [slice(start, start + size) for start in range(0, count, size)]


def started(copies):
    for copy in copies:
        copy.start()
    return copies


def waited(copies):
    for copy in copies:
        copy.wait()


def load_kernel(tod_ref, *refs):
    *parts, sem = refs
    first = tod_ref.shape[1] - TAIL
    copies, done = [], 0
    for i, part in enumerate(parts):
        there = slice(done, done + part.shape[0])
        copies.append(pltpu.make_async_copy(tod_ref.at[there, first:], part, sem.at[i]))
        done = there.stop
    waited(started(copies))


def project_kernel(
    tod_ref, wt_ref, modes_ref, ids_ref, counts_ref, edges_ref, fh_ref, fl_ref,
    p_ref, vt_ref, mask_ref,
):
    segs = p_ref.shape[0]
    counts = counts_ref[...]
    mask = band_rows(edges_ref[...], 2 * BINS)
    mask_ref[...] = mask
    vts = []
    for here in rows_of(modes_ref):
        wt = wt_ref[:, here]
        modes_t = modes_ref[here, :].T
        row = lax.broadcasted_iota(jnp.int32, (KMAX, here.stop - here.start), 0)
        mine = row == ids_ref[:, here]
        parts = []
        for b in range(BANDS):
            part = jnp.where(row < counts[:, b : b + 1], modes_t[b * KMAX : (b + 1) * KMAX], 0.0)
            parts.append(part * wt[b : b + 1])
        for b in range(BANDS):
            parts.append(jnp.where(mine, wt[b : b + 1], 0.0))
        vts.append(jnp.concatenate(parts, 0))
        vt_ref[:, here] = vts[-1]
    vt = split(jnp.concatenate(vts, 1))
    q = [dot3(vt, split(tod_ref[:, j * STEP : (j + 1) * STEP])) for j in range(segs)]
    g = dot3(split(jnp.concatenate(q, 0)), (fh_ref[...], fl_ref[...]))
    for j in range(segs):
        for part_idx in range(2):
            total = 0.0
            for b in range(BANDS):
                at = j * COLS + part_idx * MODES + b * KMAX
                total += mask[b : b + 1] * g[at : at + KMAX]
            p_ref[j, part_idx * KMAX : (part_idx + 1) * KMAX, :] = total


def prepare_kernel(vt_ref, wt_ref, mask_ref, coef_ref, v_ref, w_ref, levels_ref):
    mask = jnp.concatenate([mask_ref[...]] * 3, 0).astype(BF16)
    across = (((0,), (0,)), ((), ()))
    levels_ref[...] = lax.dot_general(
        three(coef_ref[...]), mask, across, preferred_element_type=F32
    )
    one_each = jnp.concatenate([mask[:, :HALF], mask[:, BINS : BINS + HALF]], 1)
    for here in rows_of(v_ref):
        v_ref[here, :COLS], v_ref[here, COLS:] = split(vt_ref[:, here].T)
        w_ref[here, :] = lax.dot_general(
            three(wt_ref[:, here]), one_each, across, preferred_element_type=F32
        )


def filtered(pairs, w, tables):
    fh, fl, ih, il = tables
    sums = split(jnp.concatenate([early + late for early, late in pairs], 0))
    gaps = split(jnp.concatenate([early - late for early, late in pairs], 0))
    even = dot3(sums, (fh[:, :BINS], fl[:, :BINS]))
    odd = dot3(gaps, (fh[:, BINS:], fl[:, BINS:]))
    we = jnp.concatenate([jnp.concatenate([w[:, :HALF]] * 2, 1)] * len(pairs), 0)
    wo = jnp.concatenate([jnp.concatenate([w[:, HALF:]] * 2, 1)] * len(pairs), 0)
    return dot3(split(even * we), (ih[:BINS], il[:BINS])) + dot3(
        split(odd * wo), (ih[BINS:], il[BINS:])
    )


def main_kernel(tod_ref, w_ref, fh_ref, fl_ref, ih_ref, il_ref, out_ref):
    tables = fh_ref[...], fl_ref[...], ih_ref[...], il_ref[...]
    for here in rows_of(tod_ref, 512):
        blocks = [tod_ref[here, at : at + STEP] for at in range(0, tod_ref.shape[1], STEP)]
        y = filtered(list(zip(blocks, blocks[1:])), w_ref[here, :], tables)
        chunk = here.stop - here.start
        for seg in range(len(blocks) - 1):
            out_ref[here, seg * STEP : (seg + 1) * STEP] = y[seg * chunk : (seg + 1) * chunk]


def pack_kernel(tail_ref, p_ref, q_ref, out_ref):
    count = tail_ref.shape[0]
    out_ref[:count, :] = tail_ref[...]
    sums = p_ref[p_ref.shape[0] - 1] + q_ref[q_ref.shape[0] - 1]
    out_ref[count : count + ROWS, :] = sums[:, :BINS]
    out_ref[count + ROWS :, :] = sums[:, BINS:]


def to_correct(mask, before, after, core, levels):
    sums = jnp.concatenate(
        [before[:, :BINS] + after[:, :BINS], before[:, BINS:] - after[:, BINS:]], 1
    )
    core = jnp.concatenate([core[b] for b in range(BANDS)], 0)
    mixed = dot3(split(core), split(sums[:KMAX]))
    blocks = levels * sums[KMAX:]
    masks = [mask[b : b + 1] for b in range(BANDS)]
    parts = [masks[b] * mixed[b * KMAX : (b + 1) * KMAX] for b in range(BANDS)]
    return jnp.concatenate(parts + [masks[b] * blocks for b in range(BANDS)], 0)


def rest_kernel(
    main_ref, p_ref, q_ref, v_ref, mask_ref, levels_ref, core_ref, ih_ref, il_ref, out_ref
):
    segs = p_ref.shape[0]
    sums = [p_ref[j] + q_ref[j] for j in range(segs)]
    mask, levels, core = mask_ref[...], levels_ref[...], core_ref[...]
    rows = [to_correct(mask, a, b, core, levels) for a, b in zip(sums, sums[1:])]
    z = dot3(split(jnp.concatenate(rows, 0)), (ih_ref[...], il_ref[...]))
    z = split(jnp.concatenate([z[g * COLS : (g + 1) * COLS] for g in range(segs - 1)], 1))
    out_ref[...] = main_ref[...] - dot3((v_ref[:, :COLS], v_ref[:, COLS:]), z)


def came(odd, even):
    place = lax.axis_index("tm")
    return jnp.where(place > 0, jnp.where(place % 2 == 1, odd, even), 0.0)


def soon_kernel(
    rest_ref, odd_ref, even_ref, tod_ref, w_ref, fh_ref, fl_ref, ih_ref, il_ref,
    whole_ref, out_ref, sem,
):
    upper = slice(0, rest_ref.shape[0] // 2)
    copy = pltpu.make_async_copy(rest_ref.at[upper, :], whole_ref.at[upper, STEP:], sem)
    copy.start()
    tables = fh_ref[...], fl_ref[...], ih_ref[...], il_ref[...]
    soon = out_ref.shape[0]
    pair = came(odd_ref[...], even_ref[...]), tod_ref[:soon, :STEP]
    out_ref[...] = filtered([pair], w_ref[:soon, :], tables)
    copy.wait()


def middle_kernel(
    _, rest_ref, soon_ref, odd_ref, even_ref, tod_ref, w_ref, p_ref, q_ref, v_ref, mask_ref,
    levels_ref, core_ref, fh_ref, fl_ref, ih_ref, il_ref, whole_ref, out_ref, off_ref, sem,
):
    lower = slice(rest_ref.shape[0] // 2, rest_ref.shape[0])
    copy = pltpu.make_async_copy(rest_ref.at[lower, :], whole_ref.at[lower, STEP:], sem)
    copy.start()
    tables = fh_ref[...], fl_ref[...], ih_ref[...], il_ref[...]
    soon, done = soon_ref.shape[0], out_ref.shape[0]
    sent = came(odd_ref[...], even_ref[...])
    before = sent[done - soon :]
    before = jnp.concatenate([before[:ROWS], before[ROWS:]], 1)
    rows = to_correct(
        mask_ref[...], before, p_ref[0] + q_ref[0], core_ref[...], levels_ref[...]
    )
    z = split(dot3(split(rows), tables[2:]))
    pair = sent[: done - soon], tod_ref[soon:done, :STEP]
    own = filtered([pair], w_ref[soon:done, :], tables)
    off = dot3((v_ref[:, :COLS], v_ref[:, COLS:]), z)
    out_ref[:soon, :] = soon_ref[...] - off[:soon]
    out_ref[soon:, :] = own - off[soon:done]
    off_ref[...] = off[done:]
    copy.wait()


def late_kernel(
    _, most_ref, off_ref, odd_ref, even_ref, tod_ref, w_ref, fh_ref, fl_ref, ih_ref, il_ref,
    out_ref, buf, sem,
):
    done = most_ref.shape[0]
    copies = [pltpu.make_async_copy(most_ref, out_ref.at[:done, :STEP], sem.at[0])]
    copies[0].start()
    tables = fh_ref[...], fl_ref[...], ih_ref[...], il_ref[...]
    pair = came(odd_ref[...], even_ref[...]), tod_ref[done:, :STEP]
    buf[...] = filtered([pair], w_ref[done:, :], tables) - off_ref[...]
    copies.append(pltpu.make_async_copy(buf, out_ref.at[done:, :STEP], sem.at[1]))
    copies[1].start()
    waited(copies)


IN_VMEM = pl.BlockSpec(memory_space=pltpu.VMEM)
ANYWHERE = pl.BlockSpec(memory_space=pl.ANY)


def run(kernel, loose, kept, outs, scratch=(), alias=None, flops=0, nbytes=0):
    loose = [pltpu.with_memory_space_constraint(a, pltpu.HBM) for a in loose]
    kept = [pltpu.with_memory_space_constraint(a, pltpu.VMEM) for a in kept]
    many = isinstance(outs, tuple)
    places = tuple(
        ANYWHERE if isinstance(o, jax.ShapeDtypeStruct) else IN_VMEM for o in (outs if many else (outs,))
    )
    return pl.pallas_call(
        kernel,
        out_shape=outs,
        in_specs=[ANYWHERE] * len(loose) + [IN_VMEM] * len(kept),
        out_specs=places if many else places[0],
        scratch_shapes=list(scratch),
        input_output_aliases=alias or {},
        cost_estimate=pl.CostEstimate(flops=flops, bytes_accessed=nbytes, transcendentals=0),
        compiler_params=pltpu.CompilerParams(vmem_limit_bytes=24 << 20),
    )(*loose, *kept)


def exchanged(block, axis, distance):
    devices = range(lax.axis_size(axis))
    return lax.ppermute(block, axis, [(i, i ^ distance) for i in devices])


def pair_swap(block, parity):
    n, m = lax.axis_size("tm"), lax.axis_size("wafer")
    route = []
    for t in range(n):
        mate = t + 1 if t % 2 == parity else t - 1
        for w in range(m):
            near = w ^ 1 if w ^ 1 < m else w
            to = (mate, w) if 0 <= mate < n else (t, near)
            route.append((t * m + w, to[0] * m + to[1]))
    return lax.ppermute(block, ("tm", "wafer"), route)


def local(tod, inv_white, modes, mode_counts, core, block_coef, block_ids, band_edges):
    dets, samples = tod.shape
    segs = samples // STEP
    known = samples - TAIL
    fh, fl, ih, il = tables = make_tables()
    late = middle = dets // 8
    soon = dets - late - middle
    whole = jax.ShapeDtypeStruct((dets, samples), F32)

    small = (
        inv_white.T,
        modes,
        block_ids.reshape(1, dets),
        mode_counts.reshape(1, BANDS),
        band_edges.reshape(1, BANDS + 1),
    )
    tails = run(
        load_kernel,
        (tod,),
        (),
        tuple(pltpu.VMEM((count, TAIL), F32) for count in (soon, middle, late)),
        scratch=[pltpu.SemaphoreType.DMA((3,))],
        flops=int(2e10),
        nbytes=8 * dets * TAIL,
    )
    odd_soon = pair_swap(tails[0], 0)
    even_soon = pair_swap(tails[0], 1)

    sums, vt, mask = run(
        project_kernel,
        (),
        (tod, *small, fh, fl),
        (
            pltpu.VMEM((segs, ROWS, 2 * BINS), F32),
            pltpu.VMEM((COLS, dets), F32),
            pltpu.VMEM((BANDS, 2 * BINS), F32),
        ),
        flops=6 * dets * COLS * samples,
        nbytes=4 * dets * samples,
    )
    v, w, levels = run(
        prepare_kernel,
        (),
        (vt, small[0], mask, block_coef),
        (
            pltpu.VMEM((dets, 2 * COLS), BF16),
            pltpu.VMEM((dets, BINS), F32),
            pltpu.VMEM((NBLK, 2 * BINS), F32),
        ),
        flops=6 * dets * COLS * BANDS,
        nbytes=8 * dets * COLS,
    )
    main = run(
        main_kernel,
        (),
        (tod, w, *tables),
        pltpu.VMEM((dets, known), F32),
        flops=24 * dets * STEP * known,
        nbytes=7 * dets * samples,
    )

    own, other, distance = sums, jnp.zeros_like(sums), 1
    while distance < lax.axis_size("wafer"):
        own = own + other if distance > 1 else own
        other = exchanged(own, "wafer", distance)
        distance *= 2

    packed = run(
        pack_kernel,
        (),
        (tails[1], own, other),
        pltpu.VMEM((middle + 2 * ROWS, TAIL), F32),
        nbytes=8 * middle * TAIL,
    )
    odd_middle = pair_swap(packed, 0)
    even_middle = pair_swap(packed, 1)
    odd_late = pair_swap(tails[2], 0)
    even_late = pair_swap(tails[2], 1)

    rest = run(
        rest_kernel,
        (),
        (main, own, other, v, mask, levels, core, ih, il),
        pltpu.VMEM((dets, known), F32),
        flops=6 * dets * COLS * known,
        nbytes=4 * dets * samples,
    )
    partly, filtered_soon = run(
        soon_kernel,
        (),
        (rest, odd_soon, even_soon, tod, w, *tables),
        (whole, pltpu.VMEM((soon, STEP), F32)),
        scratch=[pltpu.SemaphoreType.DMA],
        flops=24 * soon * STEP * STEP,
        nbytes=8 * soon * STEP,
    )
    partly, most, off = run(
        middle_kernel,
        (partly,),
        (rest, filtered_soon, odd_middle, even_middle, tod, w, own, other, v, mask, levels, core, *tables),
        (whole, pltpu.VMEM((soon + middle, STEP), F32), pltpu.VMEM((late, STEP), F32)),
        scratch=[pltpu.SemaphoreType.DMA],
        alias={0: 0},
        flops=8 * dets * STEP * STEP,
        nbytes=4 * dets * STEP,
    )
    return run(
        late_kernel,
        (partly,),
        (most, off, odd_late, even_late, tod, w, *tables),
        whole,
        scratch=[pltpu.VMEM((late, STEP), F32), pltpu.SemaphoreType.DMA((2,))],
        alias={0: 0},
        flops=24 * late * STEP * STEP,
        nbytes=8 * dets * STEP,
    )


def solution(mesh):
    return jax.shard_map(
        local,
        mesh=mesh,
        in_specs=(
            P(("real", "wafer"), "tm"),
            P("wafer", None),
            P("wafer", None),
            P(),
            P(),
            P(),
            P("wafer"),
            P(),
        ),
        out_specs=P(("real", "wafer"), "tm"),
        check_vma=False,
    )
```

```python
import math

import jax
import jax.numpy as jnp
import numpy as np
from jax import lax
from jax.experimental import pallas as pl
from jax.experimental.pallas import tpu as pltpu
from jax.sharding import PartitionSpec as P


STEP = 256
TAIL = 256
BANDS = 8
KMAX = 16
NBLK = 16
SEGLEN = 512
BINS = 256
HALF = BINS // 2
MODES = BANDS * KMAX
COLS = BANDS * (KMAX + NBLK)
ROWS = KMAX + NBLK


F32 = jnp.float32
BF16 = jnp.bfloat16


def pieces_of(table):
    high = table.astype(BF16)
    low = (table - high.astype(np.float64)).astype(BF16)
    return jnp.asarray(high), jnp.asarray(low)


def make_tables():
    bins = np.concatenate([np.arange(0, BINS, 2), np.arange(1, BINS, 2)]).reshape(2, HALF)
    time = np.arange(STEP)
    angle = 2.0 * math.pi / SEGLEN * (time[:, None, None] * bins[None] % SEGLEN)
    forward = np.stack([np.cos(angle), -np.sin(angle)], 2).reshape(STEP, 2 * BINS)
    kept = np.arange(TAIL, SEGLEN)
    back = 2.0 * math.pi / SEGLEN * (bins[:, :, None] * kept % SEGLEN)
    factor = np.where(bins == 0, 1.0, 2.0)[:, :, None] / SEGLEN
    inverse = np.stack([factor * np.cos(back), -factor * np.sin(back)], 1).reshape(2 * BINS, STEP)
    return pieces_of(forward) + pieces_of(inverse)


def split(x):
    high = x.astype(BF16)
    return high, (x - high.astype(F32)).astype(BF16)


def three(x):
    first = x.astype(BF16).astype(F32)
    second = (x - first).astype(BF16).astype(F32)
    return jnp.concatenate([first, second, x - first - second], 0).astype(BF16)


def dot(a, b):
    return jnp.dot(a, b, preferred_element_type=F32)


def dot3(a, b):
    return dot(a[0], b[0]) + (dot(a[0], b[1]) + dot(a[1], b[0]))


def band_rows(edges, width):
    col = lax.broadcasted_iota(jnp.int32, (1, width), 1)
    odd = (col >= width // 2).astype(jnp.int32)
    bin_idx = 2 * (col & (HALF - 1)) + odd
    rows = [
        (bin_idx >= edges[:, b : b + 1]) & (bin_idx < edges[:, b + 1 : b + 2])
        for b in range(BANDS)
    ]
    return jnp.concatenate([row.astype(F32) for row in rows], 0)


def chunk_of(count, most):
    return most if count % most == 0 else count


def rows_of(ref, most=256):
    count = ref.shape[0]
    size = chunk_of(count, most)
    return [slice(start, start + size) for start in range(0, count, size)]


def started(copies):
    for copy in copies:
        copy.start()
    return copies


def waited(copies):
    for copy in copies:
        copy.wait()


def tail_copies(tod_ref, start, parts, sem):
    first = tod_ref.shape[1] - TAIL
    copies = []
    for i, part in enumerate(parts):
        there = slice(start, start + part.shape[0])
        copies.append(pltpu.make_async_copy(tod_ref.at[there, first:], part, sem.at[i]))
        start = there.stop
    return started(copies)


def load_kernel(tod_ref, out_ref, sem):
    waited(tail_copies(tod_ref, 0, [out_ref], sem))


def project_kernel(
    tod_ref, wt_ref, modes_ref, ids_ref, counts_ref, edges_ref, fh_ref, fl_ref,
    p_ref, vt_ref, mask_ref,
):
    segs = p_ref.shape[0]
    counts = counts_ref[...]
    mask = band_rows(edges_ref[...], 2 * BINS)
    mask_ref[...] = mask
    vts = []
    for here in rows_of(modes_ref):
        wt = wt_ref[:, here]
        modes_t = modes_ref[here, :].T
        row = lax.broadcasted_iota(jnp.int32, (KMAX, here.stop - here.start), 0)
        mine = row == ids_ref[:, here]
        parts = []
        for b in range(BANDS):
            part = jnp.where(row < counts[:, b : b + 1], modes_t[b * KMAX : (b + 1) * KMAX], 0.0)
            parts.append(part * wt[b : b + 1])
        for b in range(BANDS):
            parts.append(jnp.where(mine, wt[b : b + 1], 0.0))
        vts.append(jnp.concatenate(parts, 0))
        vt_ref[:, here] = vts[-1]
    vt = split(jnp.concatenate(vts, 1))
    q = [dot3(vt, split(tod_ref[:, j * STEP : (j + 1) * STEP])) for j in range(segs)]
    g = dot3(split(jnp.concatenate(q, 0)), (fh_ref[...], fl_ref[...]))
    for j in range(segs):
        for part_idx in range(2):
            total = 0.0
            for b in range(BANDS):
                at = j * COLS + part_idx * MODES + b * KMAX
                total += mask[b : b + 1] * g[at : at + KMAX]
            p_ref[j, part_idx * KMAX : (part_idx + 1) * KMAX, :] = total


def prepare_kernel(
    tod_ref, vt_ref, wt_ref, mask_ref, coef_ref, v_ref, w_ref, levels_ref, middle_ref, late_ref, sem
):
    parts = [middle_ref, late_ref]
    start = tod_ref.shape[0] - sum(part.shape[0] for part in parts)
    copies = tail_copies(tod_ref, start, parts, sem)
    mask = jnp.concatenate([mask_ref[...]] * 3, 0).astype(BF16)
    across = (((0,), (0,)), ((), ()))
    levels_ref[...] = lax.dot_general(
        three(coef_ref[...]), mask, across, preferred_element_type=F32
    )
    one_each = jnp.concatenate([mask[:, :HALF], mask[:, BINS : BINS + HALF]], 1)
    for here in rows_of(v_ref):
        v_ref[here, :COLS], v_ref[here, COLS:] = split(vt_ref[:, here].T)
        w_ref[here, :] = lax.dot_general(
            three(wt_ref[:, here]), one_each, across, preferred_element_type=F32
        )
    waited(copies)


def back(spectra, ih, il):
    even = dot3(split(spectra[:, :BINS]), (ih[:BINS], il[:BINS]))
    return even + dot3(split(spectra[:, BINS:]), (ih[BINS:], il[BINS:]))


def filtered(pairs, w, tables):
    fh, fl, ih, il = tables
    sums = split(jnp.concatenate([early + late for early, late in pairs], 0))
    gaps = split(jnp.concatenate([early - late for early, late in pairs], 0))
    even = dot3(sums, (fh[:, :BINS], fl[:, :BINS]))
    odd = dot3(gaps, (fh[:, BINS:], fl[:, BINS:]))
    we = jnp.concatenate([jnp.concatenate([w[:, :HALF]] * 2, 1)] * len(pairs), 0)
    wo = jnp.concatenate([jnp.concatenate([w[:, HALF:]] * 2, 1)] * len(pairs), 0)
    return dot3(split(even * we), (ih[:BINS], il[:BINS])) + dot3(
        split(odd * wo), (ih[BINS:], il[BINS:])
    )


def main_kernel(tod_ref, w_ref, fh_ref, fl_ref, ih_ref, il_ref, out_ref):
    tables = fh_ref[...], fl_ref[...], ih_ref[...], il_ref[...]
    for here in rows_of(tod_ref, 512):
        blocks = [tod_ref[here, at : at + STEP] for at in range(0, tod_ref.shape[1], STEP)]
        y = filtered(list(zip(blocks, blocks[1:])), w_ref[here, :], tables)
        chunk = here.stop - here.start
        for seg in range(len(blocks) - 1):
            out_ref[here, seg * STEP : (seg + 1) * STEP] = y[seg * chunk : (seg + 1) * chunk]


def pack_kernel(tail_ref, p_ref, q_ref, out_ref):
    count = tail_ref.shape[0]
    out_ref[:count, :] = tail_ref[...]
    sums = p_ref[p_ref.shape[0] - 1] + q_ref[q_ref.shape[0] - 1]
    out_ref[count : count + ROWS, :] = sums[:, :BINS]
    out_ref[count + ROWS :, :] = sums[:, BINS:]


def to_correct(mask, before, after, core, levels):
    sums = jnp.concatenate(
        [before[:, :BINS] + after[:, :BINS], before[:, BINS:] - after[:, BINS:]], 1
    )
    core = jnp.concatenate([core[b] for b in range(BANDS)], 0)
    mixed = dot3(split(core), split(sums[:KMAX]))
    blocks = levels * sums[KMAX:]
    masks = [mask[b : b + 1] for b in range(BANDS)]
    parts = [masks[b] * mixed[b * KMAX : (b + 1) * KMAX] for b in range(BANDS)]
    return jnp.concatenate(parts + [masks[b] * blocks for b in range(BANDS)], 0)


def rest_kernel(
    main_ref, p_ref, q_ref, v_ref, mask_ref, levels_ref, core_ref, ih_ref, il_ref, out_ref
):
    segs = p_ref.shape[0]
    sums = [p_ref[j] + q_ref[j] for j in range(segs)]
    mask, levels, core = mask_ref[...], levels_ref[...], core_ref[...]
    rows = [to_correct(mask, a, b, core, levels) for a, b in zip(sums, sums[1:])]
    z = split(back(jnp.concatenate(rows, 0), ih_ref[...], il_ref[...]))
    for g in range(segs - 1):
        own = z[0][g * COLS : (g + 1) * COLS], z[1][g * COLS : (g + 1) * COLS]
        cols = slice(g * STEP, (g + 1) * STEP)
        for here in rows_of(out_ref, 512):
            off = dot3((v_ref[here, :COLS], v_ref[here, COLS:]), own)
            out_ref[here, cols] = main_ref[here, cols] - off


def came(odd, even):
    place = lax.axis_index("tm")
    return jnp.where(place > 0, jnp.where(place % 2 == 1, odd, even), 0.0)


def soon_kernel(
    rest_ref, odd_ref, even_ref, tod_ref, w_ref, fh_ref, fl_ref, ih_ref, il_ref,
    whole_ref, out_ref, sem,
):
    upper = slice(0, rest_ref.shape[0] // 2)
    copy = pltpu.make_async_copy(rest_ref.at[upper, :], whole_ref.at[upper, STEP:], sem)
    copy.start()
    tables = fh_ref[...], fl_ref[...], ih_ref[...], il_ref[...]
    soon = out_ref.shape[0]
    pair = came(odd_ref[...], even_ref[...]), tod_ref[:soon, :STEP]
    out_ref[...] = filtered([pair], w_ref[:soon, :], tables)
    copy.wait()


def middle_kernel(
    _, rest_ref, soon_ref, odd_ref, even_ref, tod_ref, w_ref, p_ref, q_ref, v_ref, mask_ref,
    levels_ref, core_ref, fh_ref, fl_ref, ih_ref, il_ref, whole_ref, out_ref, off_ref, sem,
):
    lower = slice(rest_ref.shape[0] // 2, rest_ref.shape[0])
    copy = pltpu.make_async_copy(rest_ref.at[lower, :], whole_ref.at[lower, STEP:], sem)
    copy.start()
    tables = fh_ref[...], fl_ref[...], ih_ref[...], il_ref[...]
    soon, done = soon_ref.shape[0], out_ref.shape[0]
    sent = came(odd_ref[...], even_ref[...])
    before = sent[done - soon :]
    before = jnp.concatenate([before[:ROWS], before[ROWS:]], 1)
    rows = to_correct(
        mask_ref[...], before, p_ref[0] + q_ref[0], core_ref[...], levels_ref[...]
    )
    z = split(back(rows, *tables[2:]))
    pair = sent[: done - soon], tod_ref[soon:done, :STEP]
    own = filtered([pair], w_ref[soon:done, :], tables)
    half = soon // 2
    for here in (slice(0, half), slice(half, soon)):
        out_ref[here, :] = soon_ref[here, :] - dot3((v_ref[here, :COLS], v_ref[here, COLS:]), z)
    off = dot3((v_ref[soon:, :COLS], v_ref[soon:, COLS:]), z)
    out_ref[soon:, :] = own - off[: done - soon]
    off_ref[...] = off[done - soon :]
    copy.wait()


def late_kernel(
    _, most_ref, off_ref, odd_ref, even_ref, tod_ref, w_ref, fh_ref, fl_ref, ih_ref, il_ref,
    out_ref, buf, sem,
):
    done = most_ref.shape[0]
    copies = [pltpu.make_async_copy(most_ref, out_ref.at[:done, :STEP], sem.at[0])]
    copies[0].start()
    tables = fh_ref[...], fl_ref[...], ih_ref[...], il_ref[...]
    pair = came(odd_ref[...], even_ref[...]), tod_ref[done:, :STEP]
    buf[...] = filtered([pair], w_ref[done:, :], tables) - off_ref[...]
    copies.append(pltpu.make_async_copy(buf, out_ref.at[done:, :STEP], sem.at[1]))
    copies[1].start()
    waited(copies)


IN_VMEM = pl.BlockSpec(memory_space=pltpu.VMEM)
ANYWHERE = pl.BlockSpec(memory_space=pl.ANY)


def run(kernel, loose, kept, outs, scratch=(), alias=None, flops=0, nbytes=0):
    loose = [pltpu.with_memory_space_constraint(a, pltpu.HBM) for a in loose]
    kept = [pltpu.with_memory_space_constraint(a, pltpu.VMEM) for a in kept]
    many = isinstance(outs, tuple)
    places = tuple(
        ANYWHERE if isinstance(o, jax.ShapeDtypeStruct) else IN_VMEM for o in (outs if many else (outs,))
    )
    return pl.pallas_call(
        kernel,
        out_shape=outs,
        in_specs=[ANYWHERE] * len(loose) + [IN_VMEM] * len(kept),
        out_specs=places if many else places[0],
        scratch_shapes=list(scratch),
        input_output_aliases=alias or {},
        cost_estimate=pl.CostEstimate(flops=flops, bytes_accessed=nbytes, transcendentals=0),
        compiler_params=pltpu.CompilerParams(vmem_limit_bytes=24 << 20),
    )(*loose, *kept)


def exchanged(block, axis, distance):
    devices = range(lax.axis_size(axis))
    return lax.ppermute(block, axis, [(i, i ^ distance) for i in devices])


def pair_swap(block, parity):
    n, m = lax.axis_size("tm"), lax.axis_size("wafer")
    route = []
    for t in range(n):
        mate = t + 1 if t % 2 == parity else t - 1
        for w in range(m):
            near = w ^ 1 if w ^ 1 < m else w
            to = (mate, w) if 0 <= mate < n else (t, near)
            route.append((t * m + w, to[0] * m + to[1]))
    return lax.ppermute(block, ("tm", "wafer"), route)


def local(tod, inv_white, modes, mode_counts, core, block_coef, block_ids, band_edges):
    dets, samples = tod.shape
    segs = samples // STEP
    known = samples - TAIL
    fh, fl, ih, il = tables = make_tables()
    late, middle = dets // 8, dets // 16
    soon = dets - late - middle
    whole = jax.ShapeDtypeStruct((dets, samples), F32)

    small = (
        inv_white.T,
        modes,
        block_ids.reshape(1, dets),
        mode_counts.reshape(1, BANDS),
        band_edges.reshape(1, BANDS + 1),
    )
    tail = run(
        load_kernel,
        (tod,),
        (),
        pltpu.VMEM((soon, TAIL), F32),
        scratch=[pltpu.SemaphoreType.DMA((1,))],
        flops=int(2e10),
        nbytes=8 * soon * TAIL,
    )
    odd_soon = pair_swap(tail, 0)
    even_soon = pair_swap(tail, 1)

    sums, vt, mask = run(
        project_kernel,
        (),
        (tod, *small, fh, fl),
        (
            pltpu.VMEM((segs, ROWS, 2 * BINS), F32),
            pltpu.VMEM((COLS, dets), F32),
            pltpu.VMEM((BANDS, 2 * BINS), F32),
        ),
        flops=6 * dets * COLS * samples,
        nbytes=4 * dets * samples,
    )
    v, w, levels, middle_tail, late_tail = run(
        prepare_kernel,
        (tod,),
        (vt, small[0], mask, block_coef),
        (
            pltpu.VMEM((dets, 2 * COLS), BF16),
            pltpu.VMEM((dets, BINS), F32),
            pltpu.VMEM((NBLK, 2 * BINS), F32),
            pltpu.VMEM((middle, TAIL), F32),
            pltpu.VMEM((late, TAIL), F32),
        ),
        scratch=[pltpu.SemaphoreType.DMA((2,))],
        flops=6 * dets * COLS * BANDS,
        nbytes=8 * dets * COLS,
    )
    main = run(
        main_kernel,
        (),
        (tod, w, *tables),
        pltpu.VMEM((dets, known), F32),
        flops=24 * dets * STEP * known,
        nbytes=7 * dets * samples,
    )

    own, other, distance = sums, jnp.zeros_like(sums), 1
    while distance < lax.axis_size("wafer"):
        own = own + other if distance > 1 else own
        other = exchanged(own, "wafer", distance)
        distance *= 2

    packed = run(
        pack_kernel,
        (),
        (middle_tail, own, other),
        pltpu.VMEM((middle + 2 * ROWS, TAIL), F32),
        nbytes=8 * middle * TAIL,
    )
    odd_middle = pair_swap(packed, 0)
    even_middle = pair_swap(packed, 1)
    odd_late = pair_swap(late_tail, 0)
    even_late = pair_swap(late_tail, 1)

    rest = run(
        rest_kernel,
        (),
        (main, own, other, v, mask, levels, core, ih, il),
        pltpu.VMEM((dets, known), F32),
        flops=6 * dets * COLS * known,
        nbytes=4 * dets * samples,
    )
    partly, filtered_soon = run(
        soon_kernel,
        (),
        (rest, odd_soon, even_soon, tod, w, *tables),
        (whole, pltpu.VMEM((soon, STEP), F32)),
        scratch=[pltpu.SemaphoreType.DMA],
        flops=24 * soon * STEP * STEP,
        nbytes=8 * soon * STEP,
    )
    partly, most, off = run(
        middle_kernel,
        (partly,),
        (rest, filtered_soon, odd_middle, even_middle, tod, w, own, other, v, mask, levels, core, *tables),
        (whole, pltpu.VMEM((soon + middle, STEP), F32), pltpu.VMEM((late, STEP), F32)),
        scratch=[pltpu.SemaphoreType.DMA],
        alias={0: 0},
        flops=8 * dets * STEP * STEP,
        nbytes=4 * dets * STEP,
    )
    return run(
        late_kernel,
        (partly,),
        (most, off, odd_late, even_late, tod, w, *tables),
        whole,
        scratch=[pltpu.VMEM((late, STEP), F32), pltpu.SemaphoreType.DMA((2,))],
        alias={0: 0},
        flops=24 * late * STEP * STEP,
        nbytes=8 * dets * STEP,
    )


def solution(mesh):
    return jax.shard_map(
        local,
        mesh=mesh,
        in_specs=(
            P(("real", "wafer"), "tm"),
            P("wafer", None),
            P("wafer", None),
            P(),
            P(),
            P(),
            P("wafer"),
            P(),
        ),
        out_specs=P(("real", "wafer"), "tm"),
        check_vma=False,
    )
```
